32 devices in a mesh: ctx: 8 (over z, x), head: 4 (over y, core).
Axes of the slice: x: 2, y: 2, z: 4, core: 2. Of those that a mesh axis runs over, the one named last changes fastest.
Arguments:
- query: bfloat16 [8, 2, 128, 8192], P('ctx', None, 'head'), may hold values from -200 to 200
- keyval: bfloat16 [8, 2, 2, 128, 1024], P('ctx', None, None, 'head'), may hold values from -6 to 6
- doc_blocks: int32 [4], replicated, may hold values from 1 to 12, 16 in all
Outputs:
- attended: bfloat16 [8, 2, 128, 8192], P('ctx', None, 'head')
The draws below stay inside these ranges and needn't reach their ends.
Inputs may be any that keep to these rules, and one draw needn't show every extreme that they name: `doc_blocks`: documents fill the sequence in order; the longest has exactly 12 blocks.
All inputs are finite; a program needn't handle non-finite values.
Results may differ from the reference program's by a relative error of at most 0.0038.
Values may be sent and summed in bfloat16 or wider, within the bound.
A program may use at most 64 MiB of HBM per device.

```python
import math
import jax
import jax.numpy as jnp
import numpy as np
from jax import lax

QUERY_HEADS = 64
KEY_VALUE_HEADS = 8
HEAD_WIDTH = 128
CH = 128
BLK = 128
NDOC = 4
SPANS = 8
PACKED_TOKENS = 2048
SB = 16
MOSTB = 12


def refold_drawn(sequence):
    width = sequence.shape[-1]
    half_len = sequence.shape[0] // 2
    lower_half = sequence[:half_len].reshape(SPANS, CH, width)
    upper_half = jnp.flip(sequence[half_len:].reshape(SPANS, CH, width), axis=0)
    return jnp.stack([lower_half, upper_half], axis=1)


def keys_values(key):
    drawn_sample = jax.random.normal(jax.random.fold_in(key, 11), (2, PACKED_TOKENS, KEY_VALUE_HEADS * HEAD_WIDTH), jnp.float32)
    drawn_sample = jnp.clip(drawn_sample, -5.0, 5.0)
    return drawn_sample


def draw_keyval(key, part):
    drawn_sample = keys_values(key)
    return jnp.stack([refold_drawn(drawn_sample[0]), refold_drawn(drawn_sample[1])], axis=1).astype(jnp.bfloat16)


def draw_query(key, part):
    drawn_sample = jax.random.normal(jax.random.fold_in(key, 21), (PACKED_TOKENS, QUERY_HEADS * HEAD_WIDTH), jnp.float32)
    drawn_sample = jnp.clip(drawn_sample, -5.0, 5.0)
    return refold_drawn(drawn_sample).astype(jnp.bfloat16)


def split_up(number_of, total, reach, skew):
    portions = [(1 << 20) // math.isqrt(grade ** skew) + 1 for grade in range(2, number_of + 1)]
    rest, given = total - reach - (number_of - 1), [1] * (number_of - 1)
    while rest > 0:
        free = [i for i in range(number_of - 1) if given[i] < reach]
        whole, remaining = sum([portions[i] for i in free]), rest
        for i in free:
            addition = min(reach - given[i], max(1, remaining * portions[i] // whole), rest)
            given[i] = given[i] + addition
            rest = rest - addition
    return np.array([reach] + given)


def uneven(key, amount, total, limit, lean):
    if amount == 2:
        one = jax.random.randint(key, (), max(1, total - limit), min(limit, total - 1) + 1)
        return jnp.stack([one, total - one])
    tallies = jnp.asarray(split_up(amount, total, limit, lean), jnp.int32)
    couples = (amount - 1) // 2
    source_of, receiver = tallies[1:1 + 2 * couples:2], tallies[2:2 + 2 * couples:2]
    slack = jnp.minimum(source_of - 1, limit - receiver)
    moved = jax.random.randint(jax.random.fold_in(key, 1), (couples,), 0, 1 << 20) % (slack + 1)
    tallies = tallies.at[1:1 + 2 * couples:2].set(source_of - moved).at[2:2 + 2 * couples:2].set(receiver + moved)
    return tallies[jax.random.permutation(jax.random.fold_in(key, 2), amount)]


def setup_inputs(seed: int = 0) -> dict:
    arg_keys = jax.random.split(jax.random.key(seed), 4)
    query = draw_query(jax.random.fold_in(arg_keys[3], 71), 0)
    keyval = draw_keyval(jax.random.fold_in(arg_keys[3], 71), 0)
    doc_blocks = uneven(arg_keys[2], NDOC, SB, MOSTB, 2).astype(jnp.int32)
    return dict(query=query, keyval=keyval, doc_blocks=doc_blocks)


def unfold(folded):
    width = folded.shape[-1]
    lower_half = folded[:, 0].reshape(-1, width)
    upper_half = jnp.flip(folded[:, 1], axis=0).reshape(-1, width)
    return jnp.concatenate([lower_half, upper_half], axis=0)


def refold(sequence):
    width = sequence.shape[-1]
    half_len = sequence.shape[0] // 2
    lower_half = sequence[:half_len].reshape(SPANS, CH, width)
    upper_half = jnp.flip(sequence[half_len:].reshape(SPANS, CH, width), axis=0)
    return jnp.stack([lower_half, upper_half], axis=1)


def doc_index(positions, doc_ends):
    return jnp.sum((positions[:, None] >= doc_ends[None, :]).astype(jnp.int32), axis=1).astype(jnp.int32)


def reference(query, keyval, doc_blocks):
    queries_seq = unfold(query)
    keys_seq = unfold(keyval[:, 0])
    values_seq = unfold(keyval[:, 1])
    doc_ends = (jnp.cumsum(doc_blocks) * BLK).astype(jnp.int32)
    positions = jnp.arange(PACKED_TOKENS, dtype=jnp.int32)
    doc_ids = doc_index(positions, doc_ends)
    rows_per_block = min(512, PACKED_TOKENS)
    block_count = PACKED_TOKENS // rows_per_block
    heads_per_group = QUERY_HEADS // KEY_VALUE_HEADS
    scale_factor = HEAD_WIDTH ** -0.5

    def one_block(block_no):
        row_start = (block_no * rows_per_block).astype(jnp.int32)
        query_block_size = lax.dynamic_slice_in_dim(queries_seq, row_start, rows_per_block, 0)
        query_block_size = query_block_size.reshape(rows_per_block, KEY_VALUE_HEADS, heads_per_group, HEAD_WIDTH).astype(jnp.float32)
        query_pos = row_start + jnp.arange(rows_per_block, dtype=jnp.int32)
        query_doc = lax.dynamic_slice_in_dim(doc_ids, row_start, rows_per_block, 0)
        visible = (query_doc[:, None] == doc_ids[None, :]) & (positions[None, :] <= query_pos[:, None])

        def single_head(head_no):
            offset = (head_no * HEAD_WIDTH).astype(jnp.int32)
            head_keys = lax.dynamic_slice_in_dim(keys_seq, offset, HEAD_WIDTH, 1).astype(jnp.float32)
            head_values = lax.dynamic_slice_in_dim(values_seq, offset, HEAD_WIDTH, 1).astype(jnp.float32)
            head_q = query_block_size[:, head_no]
            scores = jnp.einsum("rjd,kd->jrk", head_q, head_keys) * scale_factor
            scores = jnp.where(visible[None], scores, -jnp.inf)
            row_max = jnp.max(scores, axis=-1, keepdims=True)
            probs = jnp.exp(scores - row_max)
            totals = jnp.sum(probs, axis=-1, keepdims=True)
            weights = lax.optimization_barrier(probs.astype(jnp.bfloat16)).astype(jnp.float32)
            mixed = jnp.einsum("jrk,kd->jrd", weights, head_values) / totals
            return mixed.astype(jnp.bfloat16)

        head_stack = lax.map(single_head, jnp.arange(KEY_VALUE_HEADS, dtype=jnp.int32))
        return jnp.transpose(head_stack, (2, 0, 1, 3)).reshape(rows_per_block, QUERY_HEADS * HEAD_WIDTH)

    blocks = lax.map(one_block, jnp.arange(block_count, dtype=jnp.int32))
    return refold(blocks.reshape(PACKED_TOKENS, QUERY_HEADS * HEAD_WIDTH))
```

```python
import functools
import math

import jax
import jax.numpy as jnp
from jax import lax
from jax.experimental import pallas as pl
from jax.experimental.pallas import tpu as pltpu
from jax.sharding import PartitionSpec as P

QUERY_HEADS = 64
KEY_VALUE_HEADS = 8
HEAD_WIDTH = 128
BLK = 128
MESH = pl.DeviceIdType.MESH
LOW = -1e30


def ring_place(c, n):
    return jnp.where(c % 2 == 0, c // 2, n - 1 - c // 2)


def ring_member(p, n):
    return jnp.where(p < n // 2, 2 * p, 2 * (n - 1 - p) + 1)


def gather_kernel(n, heads, q_ref, kv_ref, qo_ref, kvo_ref, q_own, kv_own,
                  local_sem, q_send, q_recv, kv_send, kv_recv, ring_send, ring_recv):
    me_c, me_h = lax.axis_index("ctx"), lax.axis_index("head")
    tokens = q_ref.shape[2]
    q_width, kv_width = qo_ref.shape[2], kvo_ref.shape[3]
    place = ring_place(me_c, n)
    right = ring_member((place + 1) % n, n)
    left = ring_member((place + n - 1) % n, n)

    own_q = pltpu.make_async_copy(
        q_ref.at[0, :, :, pl.ds(pl.multiple_of(me_h * q_width, q_width), q_width)], q_own, local_sem.at[0])
    own_kv = pltpu.make_async_copy(
        kv_ref.at[0, :, :, :, pl.ds(pl.multiple_of(me_h * kv_width, kv_width), kv_width)], kv_own, local_sem.at[1])
    own_kv.start()
    own_q.start()

    barrier = pltpu.get_barrier_semaphore()
    for d in range(1, heads):
        pl.semaphore_signal(barrier, inc=1, device_id={"head": (me_h + d) % heads}, device_id_type=MESH)
    for c in (left, right):
        pl.semaphore_signal(barrier, inc=1, device_id={"ctx": c}, device_id_type=MESH)
    pl.semaphore_wait(barrier, heads - 1 + 2)

    row0 = pl.multiple_of(me_h * tokens, tokens)
    blocks = (me_c, 2 * n - 1 - me_c)
    kv_copies, q_copies = [], []
    for d in range(1, heads):
        peer = (me_h + d) % heads
        for h in range(2):
            copy = pltpu.make_async_remote_copy(
                src_ref=kv_ref.at[0, :, h, :, pl.ds(pl.multiple_of(peer * kv_width, kv_width), kv_width)],
                dst_ref=kvo_ref.at[:, blocks[h], pl.ds(row0, tokens), :],
                send_sem=kv_send.at[d - 1, h], recv_sem=kv_recv.at[d - 1, h],
                device_id={"head": peer}, device_id_type=MESH)
            copy.start()
            kv_copies.append(copy)
    for d in range(1, heads):
        peer = (me_h + d) % heads
        copy = pltpu.make_async_remote_copy(
            src_ref=q_ref.at[0, :, :, pl.ds(pl.multiple_of(peer * q_width, q_width), q_width)],
            dst_ref=qo_ref.at[:, pl.ds(row0, tokens), :],
            send_sem=q_send.at[d - 1], recv_sem=q_recv.at[d - 1],
            device_id={"head": peer}, device_id_type=MESH)
        copy.start()
        q_copies.append(copy)

    own_kv.wait()
    puts = []
    for h in range(2):
        put = pltpu.make_async_copy(kv_own.at[:, h], kvo_ref.at[:, blocks[h], pl.ds(row0, tokens), :],
                                    local_sem.at[2 + h])
        put.start()
        puts.append(put)
    own_q.wait()
    put_q = pltpu.make_async_copy(q_own, qo_ref.at[:, pl.ds(row0, tokens), :], local_sem.at[4])
    put_q.start()
    for put in puts:
        put.wait()
    for copy in kv_copies:
        copy.wait_recv()

    def hop(step, a, h):
        origin = ring_member((place + n - step) % n if a == 0 else (place + step) % n, n)
        block = origin if h == 0 else 2 * n - 1 - origin
        return pltpu.make_async_remote_copy(
            src_ref=kvo_ref.at[a, block], dst_ref=kvo_ref.at[a, block],
            send_sem=ring_send.at[step, a, h], recv_sem=ring_recv.at[step, a, h],
            device_id={"ctx": right if a == 0 else left}, device_id_type=MESH)

    hops = []
    for step in range(n - 1):
        now = []
        for h in range(2):
            for a in range(2):
                if step > 0:
                    hops[step - 1][2 * h + a].wait_recv()
                copy = hop(step, a, h)
                copy.start()
                now.append(copy)
        hops.append(now)
    for copy in hops[-1]:
        copy.wait_recv()
    for now in hops:
        for copy in now:
            copy.wait_send()
    for copy in kv_copies:
        copy.wait_send()
    put_q.wait()
    for copy in q_copies:
        copy.wait_recv()
        copy.wait_send()


def attend_kernel(n, groups, per_group, docs_ref, where_ref, q_ref, kv_ref, o_ref, m_ref, l_ref, acc_ref):
    half = pl.program_id(0)
    span = q_ref.shape[1]
    c = where_ref[0]
    block = jnp.where(half == 0, c, 2 * n - 1 - c)
    first = jnp.int32(0)
    end = jnp.int32(0)
    for j in range(docs_ref.shape[0]):
        end = end + docs_ref[j]
        first = jnp.where(end <= block, end, first)
    factor = HEAD_WIDTH ** -0.5 * math.log2(math.e)
    pair = 2
    rows = pair * span
    lanes = HEAD_WIDTH

    for g in range(groups):
        def queries(t):
            base = (g * per_group + t * pair) * HEAD_WIDTH
            return jnp.concatenate(
                [q_ref[0, :, base + j * HEAD_WIDTH: base + (j + 1) * HEAD_WIDTH] for j in range(pair)], axis=0)

        def keyval(a, at, count):
            out = kv_ref[a, pl.ds(at, count), :, g * HEAD_WIDTH:(g + 1) * HEAD_WIDTH]
            return out.reshape(count * span, HEAD_WIDTH)

        def scores_of(t, keys):
            return lax.dot_general(queries(t), keys, (((1,), (1,)), ((), ())),
                                   preferred_element_type=jnp.float32)

        def lane_sums(p):
            total = p[:, :lanes]
            for i in range(1, p.shape[1] // lanes):
                total = total + p[:, i * lanes:(i + 1) * lanes]
            return total

        def mix(p, values):
            return lax.dot_general(p.astype(jnp.bfloat16), values, (((1,), (0,)), ((), ())),
                                   preferred_element_type=jnp.float32)

        tiles = per_group // pair
        keys, values = keyval(0, block, 1), keyval(1, block, 1)
        row_at = lax.broadcasted_iota(jnp.int32, (rows, span), 0) % span
        seen = lax.broadcasted_iota(jnp.int32, (rows, span), 1) <= row_at
        for t in range(tiles):
            s = jnp.where(seen, scores_of(t, keys), LOW)
            m = jnp.max(s, axis=-1, keepdims=True)
            p = jnp.exp2((s - m) * factor)
            m_ref[t] = jnp.broadcast_to(m, (rows, lanes))
            l_ref[t] = lane_sums(p)
            acc_ref[t] = mix(p, values)

        def fold(at, count):
            keys, values = keyval(0, at, count), keyval(1, at, count)
            for t in range(tiles):
                s = scores_of(t, keys)
                m_old = m_ref[t]
                m = jnp.maximum(m_old, jnp.max(s, axis=-1, keepdims=True))
                p = jnp.exp2((s - jnp.tile(m, (1, count * span // lanes))) * factor)
                alpha = jnp.exp2((m_old - m) * factor)
                m_ref[t] = m
                l_ref[t] = l_ref[t] * alpha + lane_sums(p)
                acc_ref[t] = acc_ref[t] * alpha + mix(p, values)

        inner = block - first

        def body(i, carry):
            fold(first + 2 * i, 2)
            return carry

        lax.fori_loop(0, inner // 2, body, 0)

        @pl.when(inner % 2 == 1)
        def _():
            fold(block - 1, 1)

        for t in range(tiles):
            out = acc_ref[t] / jnp.sum(l_ref[t], axis=-1, keepdims=True)
            out = out.astype(o_ref.dtype)
            for j in range(pair):
                base = (g * per_group + t * pair + j) * HEAD_WIDTH
                o_ref[0, :, base:base + HEAD_WIDTH] = out[j * span:(j + 1) * span]


def return_kernel(heads, o_ref, out_ref, own, local_sem, send, recv):
    me_h = lax.axis_index("head")
    tokens, width = out_ref.shape[2], o_ref.shape[2]
    take = pltpu.make_async_copy(
        o_ref.at[:, pl.ds(pl.multiple_of(me_h * tokens, tokens), tokens), :], own, local_sem.at[0])
    take.start()
    barrier = pltpu.get_barrier_semaphore()
    for d in range(1, heads):
        pl.semaphore_signal(barrier, inc=1, device_id={"head": (me_h + d) % heads}, device_id_type=MESH)
    pl.semaphore_wait(barrier, heads - 1)
    place = out_ref.at[0, :, :, pl.ds(pl.multiple_of(me_h * width, width), width)]
    copies = []
    for d in range(1, heads):
        peer = (me_h + d) % heads
        copy = pltpu.make_async_remote_copy(
            src_ref=o_ref.at[:, pl.ds(pl.multiple_of(peer * tokens, tokens), tokens), :], dst_ref=place,
            send_sem=send.at[d - 1], recv_sem=recv.at[d - 1],
            device_id={"head": peer}, device_id_type=MESH)
        copy.start()
        copies.append(copy)
    take.wait()
    put = pltpu.make_async_copy(own, place, local_sem.at[1])
    put.start()
    put.wait()
    for copy in copies:
        copy.wait()


def local(query, keyval, doc_blocks):
    n, heads = lax.axis_size("ctx"), lax.axis_size("head")
    tokens = query.shape[2]
    span = tokens * heads
    assert span == BLK
    q_width, kv_width = query.shape[3] // heads, keyval.shape[4] // heads
    groups, per_group = kv_width // HEAD_WIDTH, QUERY_HEADS // KEY_VALUE_HEADS
    kind = query.dtype
    anywhere = pl.BlockSpec(memory_space=pl.ANY)
    dma = pltpu.SemaphoreType.DMA
    rows, kv = pl.pallas_call(
        functools.partial(gather_kernel, n, heads),
        out_shape=(jax.ShapeDtypeStruct((2, span, q_width), kind),
                   jax.ShapeDtypeStruct((2, 2 * n, span, kv_width), kind)),
        in_specs=[anywhere, anywhere],
        out_specs=(anywhere, anywhere),
        scratch_shapes=[
            pltpu.VMEM((2, tokens, q_width), kind),
            pltpu.VMEM((2, 2, tokens, kv_width), kind),
            dma((5,)), dma((heads - 1,)), dma((heads - 1,)),
            dma((heads - 1, 2)), dma((heads - 1, 2)),
            dma((n - 1, 2, 2)), dma((n - 1, 2, 2)),
        ],
        compiler_params=pltpu.CompilerParams(collective_id=0, has_side_effects=True),
        name="gather",
    )(query, keyval)

    mine = jnp.reshape(lax.axis_index("ctx"), (1,)).astype(jnp.int32)
    pair_rows = 2 * span
    tiles = per_group // 2
    state = pltpu.VMEM((tiles, pair_rows, HEAD_WIDTH), jnp.float32)
    mixed = pl.pallas_call(
        functools.partial(attend_kernel, n, groups, per_group),
        out_shape=jax.ShapeDtypeStruct((2, span, q_width), kind),
        grid_spec=pltpu.PrefetchScalarGridSpec(
            num_scalar_prefetch=2, grid=(2,),
            in_specs=[pl.BlockSpec((1, span, q_width), lambda h, *_: (h, 0, 0)),
                      pl.BlockSpec((2, 2 * n, span, kv_width), lambda h, *_: (0, 0, 0, 0),
                                   pipeline_mode=pl.Buffered(1))],
            out_specs=pl.BlockSpec((1, span, q_width), lambda h, *_: (h, 0, 0)),
            scratch_shapes=[state, state, state]),
        name="attend",
    )(doc_blocks, mine, rows, kv)

    return pl.pallas_call(
        functools.partial(return_kernel, heads),
        out_shape=jax.ShapeDtypeStruct(query.shape, kind),
        in_specs=[anywhere],
        out_specs=anywhere,
        scratch_shapes=[pltpu.VMEM((2, tokens, q_width), kind), dma((2,)), dma((heads - 1,)), dma((heads - 1,))],
        compiler_params=pltpu.CompilerParams(collective_id=1, has_side_effects=True),
        name="return",
    )(mixed)


def solution(mesh):
    placed = (P("ctx", None, "head", None), P("ctx", None, None, "head", None), P())
    return jax.shard_map(
        local, mesh=mesh, in_specs=placed, out_specs=P("ctx", None, "head", None), check_vma=False
    )
```

```python
import functools
import math

import jax
import jax.numpy as jnp
from jax import lax
from jax.experimental import pallas as pl
from jax.experimental.pallas import tpu as pltpu
from jax.sharding import PartitionSpec as P

QUERY_HEADS = 64
KEY_VALUE_HEADS = 8
HEAD_WIDTH = 128
BLK = 128
MESH = pl.DeviceIdType.MESH
LOW = -1e30


def ring_place(c, n):
    return jnp.where(c % 2 == 0, c // 2, n - 1 - c // 2)


def ring_member(p, n):
    return jnp.where(p < n // 2, 2 * p, 2 * (n - 1 - p) + 1)


def fused_kernel(n, heads, per_group, docs_ref, q_ref, kv_ref, out_ref, qbuf, kvbuf, obuf, m_ref, l_ref, acc_ref,
                 own_sem, q_send, q_recv, kv_send, kv_recv, ring_send, ring_recv, o_send, o_recv):
    me_c, me_h = lax.axis_index("ctx"), lax.axis_index("head")
    tokens, half = q_ref.shape[2], n // 2
    groups, span, width = qbuf.shape[0], qbuf.shape[2], qbuf.shape[3]
    place = ring_place(me_c, n)
    right = ring_member((place + 1) % n, n)
    left = ring_member((place + n - 1) % n, n)
    mine = (me_c, 2 * n - 1 - me_c)
    row0 = pl.multiple_of(me_h * tokens, tokens)

    def q_part(peer, g):
        at = pl.multiple_of((peer * groups + g) * width, width)
        return q_ref.at[0, :, :, pl.ds(at, width)]

    def kv_part(peer, g, h):
        at = pl.multiple_of((peer * groups + g) * HEAD_WIDTH, HEAD_WIDTH)
        return kv_ref.at[0, :, h, :, pl.ds(at, HEAD_WIDTH)]

    own = []
    for g in range(groups):
        for h in range(2):
            own.append(pltpu.make_async_copy(
                kv_part(me_h, g, h), kvbuf.at[g, mine[h], :, pl.ds(row0, tokens), :], own_sem.at[3 * g + h]))
        own.append(pltpu.make_async_copy(
            q_part(me_h, g), qbuf.at[g, :, pl.ds(row0, tokens), :], own_sem.at[3 * g + 2]))
    for copy in own:
        copy.start()

    barrier = pltpu.get_barrier_semaphore()
    for d in range(1, heads):
        pl.semaphore_signal(barrier, inc=1, device_id={"head": (me_h + d) % heads}, device_id_type=MESH)
    for c in (left, right):
        pl.semaphore_signal(barrier, inc=1, device_id={"ctx": c}, device_id_type=MESH)
    pl.semaphore_wait(barrier, heads - 1 + 2)

    kv_copies = [[] for _ in range(groups)]
    q_copies = [[] for _ in range(groups)]
    for g in range(groups):
        for d in range(1, heads):
            peer = (me_h + d) % heads
            for h in range(2):
                copy = pltpu.make_async_remote_copy(
                    src_ref=kv_part(peer, g, h), dst_ref=kvbuf.at[g, mine[h], :, pl.ds(row0, tokens), :],
                    send_sem=kv_send.at[g, d - 1, h], recv_sem=kv_recv.at[g, d - 1, h],
                    device_id={"head": peer}, device_id_type=MESH)
                copy.start()
                kv_copies[g].append(copy)
    for g in range(groups):
        for d in range(1, heads):
            peer = (me_h + d) % heads
            copy = pltpu.make_async_remote_copy(
                src_ref=q_part(peer, g), dst_ref=qbuf.at[g, :, pl.ds(row0, tokens), :],
                send_sem=q_send.at[g, d - 1], recv_sem=q_recv.at[g, d - 1],
                device_id={"head": peer}, device_id_type=MESH)
            copy.start()
            q_copies[g].append(copy)

    def member_at(d, distance):
        return ring_member((place + n - distance) % n if d == 0 else (place + distance) % n, n)

    def hop(g, d, t, h):
        origin = member_at(d, t)
        block = origin if h == 0 else 2 * n - 1 - origin
        return pltpu.make_async_remote_copy(
            src_ref=kvbuf.at[g, block], dst_ref=kvbuf.at[g, block],
            send_sem=ring_send.at[g, d, t, h], recv_sem=ring_recv.at[g, d, t, h],
            device_id={"ctx": right if d == 0 else left}, device_id_type=MESH)

    def arrived(g, d, t):
        for h in range(2):
            hop(g, d, t, h).wait_recv()

    def forward(g, d, t):
        for h in range(2):
            hop(g, d, t - 1, h).wait_recv()
            hop(g, d, t, h).start()

    factor = HEAD_WIDTH ** -0.5 * math.log2(math.e)
    pair = 2
    tiles, rows = per_group // pair, pair * span

    def doc_of(block):
        end, found = jnp.int32(0), jnp.int32(0)
        for j in range(docs_ref.shape[0]):
            end = end + docs_ref[j]
            found = found + jnp.where(end <= block, 1, 0).astype(jnp.int32)
        return found

    def scores_of(g, hq, t, keys):
        base = t * pair * HEAD_WIDTH
        queries = jnp.concatenate(
            [qbuf[g, hq, :, base + j * HEAD_WIDTH: base + (j + 1) * HEAD_WIDTH] for j in range(pair)], axis=0)
        return lax.dot_general(queries, keys, (((1,), (1,)), ((), ())), preferred_element_type=jnp.float32)

    def mix(p, values):
        return lax.dot_general(p.astype(jnp.bfloat16), values, (((1,), (0,)), ((), ())),
                               preferred_element_type=jnp.float32)

    def fold(g, hq, block):
        same = doc_of(block) == doc_of(jnp.where(hq == 0, mine[0], mine[1]))
        shift = jnp.where(same, jnp.float32(0), jnp.float32(-LOW))
        keys, values = kvbuf[g, block, 0], kvbuf[g, block, 1]
        for t in range(tiles):
            s = scores_of(g, hq, t, keys)
            m_old = m_ref[hq, t]
            m = jnp.maximum(m_old, jnp.max(s, axis=-1, keepdims=True) - shift)
            p = jnp.exp2((s - (m + shift)) * factor)
            alpha = jnp.exp2((m_old - m) * factor)
            m_ref[hq, t] = m
            l_ref[hq, t] = l_ref[hq, t] * alpha + p
            acc_ref[hq, t] = acc_ref[hq, t] * alpha + mix(p, values)

    def diagonal(g):
        def each(hq, carry):
            block = jnp.where(hq == 0, mine[0], mine[1])
            keys, values = kvbuf[g, block, 0], kvbuf[g, block, 1]
            row_at = lax.broadcasted_iota(jnp.int32, (rows, span), 0) % span
            seen = lax.broadcasted_iota(jnp.int32, (rows, span), 1) <= row_at
            for t in range(tiles):
                s = jnp.where(seen, scores_of(g, hq, t, keys), LOW)
                m = jnp.max(s, axis=-1, keepdims=True)
                p = jnp.exp2((s - m) * factor)
                m_ref[hq, t] = jnp.broadcast_to(m, (rows, span))
                l_ref[hq, t] = p
                acc_ref[hq, t] = mix(p, values)
            return carry

        lax.fori_loop(0, 2, each, 0)
        fold(g, 1, mine[0])

    def absorb(g, ways, t):
        def each(k, carry):
            if len(ways) == 2:
                distance = jnp.where(k < 2, n - 1 - t, t + 1)
            else:
                distance = n - 1 - t if ways[0] == 0 else t + 1
            origin = ring_member((place + distance) % n, n)
            lower = origin < me_c
            second = k % 2 == 1
            hq = jnp.where(second & lower, 0, 1)
            block = jnp.where(second & jnp.logical_not(lower), 2 * n - 1 - origin, origin)
            fold(g, hq, block)
            return carry

        lax.fori_loop(0, 2 * len(ways), each, 0)

    back = []

    def finish(g):
        def each(hq, carry):
            for t in range(tiles):
                out = acc_ref[hq, t] / jnp.sum(l_ref[hq, t], axis=-1, keepdims=True)
                out = out.astype(obuf.dtype)
                for j in range(pair):
                    base = (t * pair + j) * HEAD_WIDTH
                    obuf[g, hq, :, base:base + HEAD_WIDTH] = out[j * span:(j + 1) * span]
            return carry

        lax.fori_loop(0, 2, each, 0)
        place_out = out_ref.at[0, :, :, pl.ds(pl.multiple_of((me_h * groups + g) * width, width), width)]
        for d in range(1, heads):
            peer = (me_h + d) % heads
            copy = pltpu.make_async_remote_copy(
                src_ref=obuf.at[g, :, pl.ds(pl.multiple_of(peer * tokens, tokens), tokens), :], dst_ref=place_out,
                send_sem=o_send.at[g, d - 1], recv_sem=o_recv.at[g, d - 1],
                device_id={"head": peer}, device_id_type=MESH)
            copy.start()
            back.append(copy)
        copy = pltpu.make_async_copy(obuf.at[g, :, pl.ds(row0, tokens), :], place_out, own_sem.at[3 * groups + g])
        copy.start()
        back.append(copy)

    def ready(g):
        for h in range(2):
            own[3 * g + h].wait()
        for copy in kv_copies[g]:
            copy.wait_recv()
        for d in range(2):
            for h in range(2):
                hop(g, d, 0, h).start()

    def queries_ready(g):
        own[3 * g + 2].wait()
        for copy in q_copies[g]:
            copy.wait_recv()

    both, two = (0, 1), groups == 2
    for g in range(groups):
        ready(g)
    queries_ready(0)
    forward(0, 0, 1)
    forward(0, 1, 1)
    diagonal(0)
    absorb(0, both, 0)

    def early(t, carry):
        forward(0, 0, t)
        forward(0, 1, t)
        absorb(0, both, t - 1)
        return carry

    lax.fori_loop(2, half - 1, early, 0)
    forward(0, 0, half - 1)
    arrived(0, 1, half - 2)
    if two:
        forward(1, 1, 1)
    absorb(0, both, half - 2)
    if two:
        forward(1, 0, 1)
        forward(1, 1, 2)
    arrived(0, 0, half - 1)
    absorb(0, (0,), half - 1)
    finish(0)

    def late(t, carry):
        forward(1, 0, t)
        forward(1, 1, t + 1)
        absorb(1, both, t - 1)
        return carry

    if two:
        queries_ready(1)
        diagonal(1)
        absorb(1, both, 0)
        lax.fori_loop(2, half - 1, late, 0)
        arrived(1, 0, half - 2)
        absorb(1, both, half - 2)
        arrived(1, 1, half - 1)
        absorb(1, (1,), half - 1)
        finish(1)

    for g in range(groups):
        for copy in kv_copies[g] + q_copies[g]:
            copy.wait_send()
        for d in range(2):
            for t in range(half if d == g else half - 1):
                for h in range(2):
                    hop(g, d, t, h).wait_send()
    for copy in back:
        copy.wait()


def local(query, keyval, doc_blocks):
    n, heads = lax.axis_size("ctx"), lax.axis_size("head")
    tokens = query.shape[2]
    span = tokens * heads
    groups, per_group = keyval.shape[4] // heads // HEAD_WIDTH, QUERY_HEADS // KEY_VALUE_HEADS
    width = per_group * HEAD_WIDTH
    assert span == BLK and groups in (1, 2) and n % 2 == 0 and n >= 8
    kind = query.dtype
    anywhere = pl.BlockSpec(memory_space=pl.ANY)
    dma = pltpu.SemaphoreType.DMA
    state = pltpu.VMEM((2, per_group // 2, 2 * span, HEAD_WIDTH), jnp.float32)
    return pl.pallas_call(
        functools.partial(fused_kernel, n, heads, per_group),
        out_shape=jax.ShapeDtypeStruct(query.shape, kind),
        in_specs=[pl.BlockSpec(memory_space=pltpu.SMEM), anywhere, anywhere],
        out_specs=anywhere,
        scratch_shapes=[
            pltpu.VMEM((groups, 2, span, width), kind),
            pltpu.VMEM((groups, 2 * n, 2, span, HEAD_WIDTH), kind),
            pltpu.VMEM((groups, 2, span, width), kind),
            state, state, state,
            dma((4 * groups,)),
            dma((groups, heads - 1)), dma((groups, heads - 1)),
            dma((groups, heads - 1, 2)), dma((groups, heads - 1, 2)),
            dma((groups, 2, n // 2, 2)), dma((groups, 2, n // 2, 2)),
            dma((groups, heads - 1)), dma((groups, heads - 1)),
        ],
        compiler_params=pltpu.CompilerParams(collective_id=0, has_side_effects=True),
        name="fused",
    )(doc_blocks, query, keyval)


def solution(mesh):
    placed = (P("ctx", None, "head", None), P("ctx", None, None, "head", None), P())
    return jax.shard_map(
        local, mesh=mesh, in_specs=placed, out_specs=P("ctx", None, "head", None), check_vma=False
    )
```

```python
import functools
import math

import jax
import jax.numpy as jnp
from jax import lax
from jax.experimental import pallas as pl
from jax.experimental.pallas import tpu as pltpu
from jax.sharding import PartitionSpec as P

QUERY_HEADS = 64
KEY_VALUE_HEADS = 8
HEAD_WIDTH = 128
BLK = 128
MESH = pl.DeviceIdType.MESH
LOW = -1e30


def ring_place(c, n):
    return jnp.where(c % 2 == 0, c // 2, n - 1 - c // 2)


def ring_member(p, n):
    return jnp.where(p < n // 2, 2 * p, 2 * (n - 1 - p) + 1)


def fused_kernel(n, heads, per_group, docs_ref, q_ref, kv_ref, out_ref, qbuf, kvbuf, obuf, m_ref, l_ref, acc_ref,
                 own_sem, q_send, q_recv, kv_send, kv_recv, ring_send, ring_recv, o_send, o_recv):
    me_c, me_h = lax.axis_index("ctx"), lax.axis_index("head")
    tokens, half = q_ref.shape[2], n // 2
    groups, span, width = qbuf.shape[0], qbuf.shape[2], qbuf.shape[3]
    place = ring_place(me_c, n)
    right = ring_member((place + 1) % n, n)
    left = ring_member((place + n - 1) % n, n)
    mine = (me_c, 2 * n - 1 - me_c)
    row0 = pl.multiple_of(me_h * tokens, tokens)

    def q_part(peer, g):
        at = pl.multiple_of((peer * groups + g) * width, width)
        return q_ref.at[0, :, :, pl.ds(at, width)]

    def kv_part(peer, g, h):
        at = pl.multiple_of((peer * groups + g) * HEAD_WIDTH, HEAD_WIDTH)
        return kv_ref.at[0, :, h, :, pl.ds(at, HEAD_WIDTH)]

    own = []
    for g in range(groups):
        for h in range(2):
            own.append(pltpu.make_async_copy(
                kv_part(me_h, g, h), kvbuf.at[g, mine[h], :, pl.ds(row0, tokens), :], own_sem.at[3 * g + h]))
        own.append(pltpu.make_async_copy(
            q_part(me_h, g), qbuf.at[g, :, pl.ds(row0, tokens), :], own_sem.at[3 * g + 2]))
    for copy in own:
        copy.start()

    barrier = pltpu.get_barrier_semaphore()
    for d in range(1, heads):
        pl.semaphore_signal(barrier, inc=1, device_id={"head": (me_h + d) % heads}, device_id_type=MESH)
    for c in (left, right):
        pl.semaphore_signal(barrier, inc=1, device_id={"ctx": c}, device_id_type=MESH)
    pl.semaphore_wait(barrier, heads - 1 + 2)

    kv_copies = [[] for _ in range(groups)]
    q_copies = [[] for _ in range(groups)]
    for g in range(groups):
        for d in range(1, heads):
            peer = (me_h + d) % heads
            for h in range(2):
                copy = pltpu.make_async_remote_copy(
                    src_ref=kv_part(peer, g, h), dst_ref=kvbuf.at[g, mine[h], :, pl.ds(row0, tokens), :],
                    send_sem=kv_send.at[g, d - 1, h], recv_sem=kv_recv.at[g, d - 1, h],
                    device_id={"head": peer}, device_id_type=MESH)
                copy.start()
                kv_copies[g].append(copy)
    for g in range(groups):
        for d in range(1, heads):
            peer = (me_h + d) % heads
            copy = pltpu.make_async_remote_copy(
                src_ref=q_part(peer, g), dst_ref=qbuf.at[g, :, pl.ds(row0, tokens), :],
                send_sem=q_send.at[g, d - 1], recv_sem=q_recv.at[g, d - 1],
                device_id={"head": peer}, device_id_type=MESH)
            copy.start()
            q_copies[g].append(copy)

    def member_at(d, distance):
        return ring_member((place + n - distance) % n if d == 0 else (place + distance) % n, n)

    def hop(g, d, t, h):
        origin = member_at(d, t)
        block = origin if h == 0 else 2 * n - 1 - origin
        return pltpu.make_async_remote_copy(
            src_ref=kvbuf.at[g, block], dst_ref=kvbuf.at[g, block],
            send_sem=ring_send.at[g, d, t, h], recv_sem=ring_recv.at[g, d, t, h],
            device_id={"ctx": right if d == 0 else left}, device_id_type=MESH)

    def arrived(g, d, t):
        for h in range(2):
            hop(g, d, t, h).wait_recv()

    def forward(g, d, t):
        for h in range(2):
            hop(g, d, t - 1, h).wait_recv()
            hop(g, d, t, h).start()

    factor = HEAD_WIDTH ** -0.5 * math.log2(math.e)
    pair = 2
    tiles, rows = per_group // pair, pair * span

    def doc_of(block):
        end, found = jnp.int32(0), jnp.int32(0)
        for j in range(docs_ref.shape[0]):
            end = end + docs_ref[j]
            found = found + jnp.where(end <= block, 1, 0).astype(jnp.int32)
        return found

    def scores_of(g, hq, t, keys):
        base = t * pair * HEAD_WIDTH
        queries = jnp.concatenate(
            [qbuf[g, hq, :, base + j * HEAD_WIDTH: base + (j + 1) * HEAD_WIDTH] for j in range(pair)], axis=0)
        return lax.dot_general(queries, keys, (((1,), (1,)), ((), ())), preferred_element_type=jnp.float32)

    def mix(p, values):
        return lax.dot_general(p.astype(jnp.bfloat16), values, (((1,), (0,)), ((), ())),
                               preferred_element_type=jnp.float32)

    def fold(g, hq, *blocks):
        doc = doc_of(jnp.where(hq == 0, mine[0], mine[1]))
        shifts = [jnp.where(doc_of(block) == doc, jnp.float32(0), jnp.float32(-LOW)) for block in blocks]
        keys = jnp.concatenate([kvbuf[g, block, 0] for block in blocks], axis=0)
        values = jnp.concatenate([kvbuf[g, block, 1] for block in blocks], axis=0)
        for t in range(tiles):
            s = scores_of(g, hq, t, keys)
            m_old = m_ref[hq, t]
            parts = [s[:, i * span:(i + 1) * span] for i in range(len(blocks))]
            top = parts[0] - shifts[0]
            for part, shift in zip(parts[1:], shifts[1:]):
                top = jnp.maximum(top, part - shift)
            m = jnp.maximum(m_old, jnp.max(top, axis=-1, keepdims=True))
            parts = [jnp.exp2((part - (m + shift)) * factor) for part, shift in zip(parts, shifts)]
            p = jnp.concatenate(parts, axis=1)
            alpha = jnp.exp2((m_old - m) * factor)
            m_ref[hq, t] = m
            l_ref[hq, t] = l_ref[hq, t] * alpha + sum(parts)
            acc_ref[hq, t] = acc_ref[hq, t] * alpha + mix(p, values)

    def diagonal(g):
        def each(hq, carry):
            block = jnp.where(hq == 0, mine[0], mine[1])
            keys, values = kvbuf[g, block, 0], kvbuf[g, block, 1]
            row_at = lax.broadcasted_iota(jnp.int32, (rows, span), 0) % span
            seen = lax.broadcasted_iota(jnp.int32, (rows, span), 1) <= row_at
            for t in range(tiles):
                s = jnp.where(seen, scores_of(g, hq, t, keys), LOW)
                m = jnp.max(s, axis=-1, keepdims=True)
                p = jnp.exp2((s - m) * factor)
                m_ref[hq, t] = jnp.broadcast_to(m, (rows, span))
                l_ref[hq, t] = p
                acc_ref[hq, t] = mix(p, values)
            return carry

        lax.fori_loop(0, 2, each, 0)
        fold(g, 1, mine[0])

    def absorb(g, ways, t):
        origins = [member_at(way, t + 1) for way in ways]
        fold(g, 1, *origins)

        def each(k, carry):
            origin = jnp.where(k == 0, origins[0], origins[-1])
            lower = origin < me_c
            fold(g, jnp.where(lower, 0, 1), jnp.where(lower, origin, 2 * n - 1 - origin))
            return carry

        lax.fori_loop(0, len(ways), each, 0)

    back = []

    def finish(g):
        cols = pl.ds(pl.multiple_of((me_h * groups + g) * width, width), width)
        for hq in range(2):
            for t in range(tiles):
                out = acc_ref[hq, t] / jnp.sum(l_ref[hq, t], axis=-1, keepdims=True)
                out = out.astype(obuf.dtype)
                for j in range(pair):
                    base = (t * pair + j) * HEAD_WIDTH
                    obuf[g, hq, :, base:base + HEAD_WIDTH] = out[j * span:(j + 1) * span]
            place_out = out_ref.at[0, hq, :, cols]
            for d in range(1, heads):
                peer = (me_h + d) % heads
                copy = pltpu.make_async_remote_copy(
                    src_ref=obuf.at[g, hq, pl.ds(pl.multiple_of(peer * tokens, tokens), tokens), :],
                    dst_ref=place_out, send_sem=o_send.at[g, hq, d - 1], recv_sem=o_recv.at[g, hq, d - 1],
                    device_id={"head": peer}, device_id_type=MESH)
                copy.start()
                back.append(copy)
            copy = pltpu.make_async_copy(obuf.at[g, hq, pl.ds(row0, tokens), :], place_out,
                                         own_sem.at[3 * groups + 2 * g + hq])
            copy.start()
            back.append(copy)

    def ready(g):
        for h in range(2):
            own[3 * g + h].wait()
        for copy in kv_copies[g]:
            copy.wait_recv()
        for d in range(2):
            for h in range(2):
                hop(g, d, 0, h).start()

    def queries_ready(g):
        own[3 * g + 2].wait()
        for copy in q_copies[g]:
            copy.wait_recv()

    both, two = (0, 1), groups == 2
    for g in range(groups):
        ready(g)
    forward(0, 0, 1)
    forward(0, 1, 1)
    queries_ready(0)
    diagonal(0)

    def early(t, carry):
        forward(0, 0, t)
        forward(0, 1, t)
        absorb(0, both, t - 2)
        return carry

    lax.fori_loop(2, half - 1, early, 0)
    forward(0, 0, half - 1)
    if two:
        forward(1, 1, 1)
    absorb(0, both, half - 3)
    if two:
        forward(1, 0, 1)
        forward(1, 1, 2)
    arrived(0, 1, half - 2)
    absorb(0, both, half - 2)
    arrived(0, 0, half - 1)
    if two:
        forward(1, 0, 2)
        forward(1, 1, 3)
    absorb(0, (0,), half - 1)
    finish(0)

    def late(t, carry):
        forward(1, 0, t)
        forward(1, 1, t + 1)
        absorb(1, both, t - 3)
        return carry

    if two:
        queries_ready(1)
        diagonal(1)
        lax.fori_loop(3, half - 1, late, 0)
        absorb(1, both, half - 4)
        absorb(1, both, half - 3)
        arrived(1, 0, half - 2)
        absorb(1, both, half - 2)
        arrived(1, 1, half - 1)
        absorb(1, (1,), half - 1)
        finish(1)

    for g in range(groups):
        for copy in kv_copies[g] + q_copies[g]:
            copy.wait_send()
        for d in range(2):
            for t in range(half if d == g else half - 1):
                for h in range(2):
                    hop(g, d, t, h).wait_send()
    for copy in back:
        copy.wait()


def local(query, keyval, doc_blocks):
    n, heads = lax.axis_size("ctx"), lax.axis_size("head")
    tokens = query.shape[2]
    span = tokens * heads
    groups, per_group = keyval.shape[4] // heads // HEAD_WIDTH, QUERY_HEADS // KEY_VALUE_HEADS
    width = per_group * HEAD_WIDTH
    assert span == BLK and groups in (1, 2) and n % 2 == 0 and n >= 8
    kind = query.dtype
    anywhere = pl.BlockSpec(memory_space=pl.ANY)
    dma = pltpu.SemaphoreType.DMA
    state = pltpu.VMEM((2, per_group // 2, 2 * span, HEAD_WIDTH), jnp.float32)
    return pl.pallas_call(
        functools.partial(fused_kernel, n, heads, per_group),
        out_shape=jax.ShapeDtypeStruct(query.shape, kind),
        in_specs=[pl.BlockSpec(memory_space=pltpu.SMEM), anywhere, anywhere],
        out_specs=anywhere,
        scratch_shapes=[
            pltpu.VMEM((groups, 2, span, width), kind),
            pltpu.VMEM((groups, 2 * n, 2, span, HEAD_WIDTH), kind),
            pltpu.VMEM((groups, 2, span, width), kind),
            state, state, state,
            dma((5 * groups,)),
            dma((groups, heads - 1)), dma((groups, heads - 1)),
            dma((groups, heads - 1, 2)), dma((groups, heads - 1, 2)),
            dma((groups, 2, n // 2, 2)), dma((groups, 2, n // 2, 2)),
            dma((groups, 2, heads - 1)), dma((groups, 2, heads - 1)),
        ],
        compiler_params=pltpu.CompilerParams(collective_id=0, has_side_effects=True),
        name="fused",
    )(doc_blocks, query, keyval)


def solution(mesh):
    placed = (P("ctx", None, "head", None), P("ctx", None, None, "head", None), P())
    return jax.shard_map(
        local, mesh=mesh, in_specs=placed, out_specs=P("ctx", None, "head", None), check_vma=False
    )
```

```python
import functools
import math

import jax
import jax.numpy as jnp
from jax import lax
from jax.experimental import pallas as pl
from jax.experimental.pallas import tpu as pltpu
from jax.sharding import PartitionSpec as P

QUERY_HEADS = 64
KEY_VALUE_HEADS = 8
HEAD_WIDTH = 128
BLK = 128
MESH = pl.DeviceIdType.MESH
LOW = -1e30


def ring_place(c, n):
    return jnp.where(c % 2 == 0, c // 2, n - 1 - c // 2)


def ring_member(p, n):
    return jnp.where(p < n // 2, 2 * p, 2 * (n - 1 - p) + 1)


def fused_kernel(n, heads, per_group, docs_ref, q_ref, kv_ref, out_ref, qbuf, kvbuf, obuf, m_ref, l_ref, acc_ref,
                 own_sem, q_send, q_recv, kv_send, kv_recv, ring_send, ring_recv, o_send, o_recv):
    me_c, me_h = lax.axis_index("ctx"), lax.axis_index("head")
    tokens, half = q_ref.shape[2], n // 2
    groups, span, width = qbuf.shape[0], qbuf.shape[2], qbuf.shape[3]
    place = ring_place(me_c, n)
    right = ring_member((place + 1) % n, n)
    left = ring_member((place + n - 1) % n, n)
    mine = (me_c, 2 * n - 1 - me_c)
    row0 = pl.multiple_of(me_h * tokens, tokens)

    def q_part(peer, g):
        at = pl.multiple_of((peer * groups + g) * width, width)
        return q_ref.at[0, :, :, pl.ds(at, width)]

    def kv_part(peer, g, h):
        at = pl.multiple_of((peer * groups + g) * HEAD_WIDTH, HEAD_WIDTH)
        return kv_ref.at[0, :, h, :, pl.ds(at, HEAD_WIDTH)]

    own = []
    for g in range(groups):
        for h in range(2):
            own.append(pltpu.make_async_copy(
                kv_part(me_h, g, h), kvbuf.at[g, mine[h], :, pl.ds(row0, tokens), :], own_sem.at[3 * g + h]))
        own.append(pltpu.make_async_copy(
            q_part(me_h, g), qbuf.at[g, :, pl.ds(row0, tokens), :], own_sem.at[3 * g + 2]))
    for copy in own:
        copy.start()

    barrier = pltpu.get_barrier_semaphore()
    for d in range(1, heads):
        pl.semaphore_signal(barrier, inc=1, device_id={"head": (me_h + d) % heads}, device_id_type=MESH)
    for c in (left, right):
        pl.semaphore_signal(barrier, inc=1, device_id={"ctx": c}, device_id_type=MESH)
    pl.semaphore_wait(barrier, heads - 1 + 2)

    kv_copies = [[] for _ in range(groups)]
    q_copies = [[] for _ in range(groups)]
    for g in range(groups):
        for d in range(1, heads):
            peer = (me_h + d) % heads
            for h in range(2):
                copy = pltpu.make_async_remote_copy(
                    src_ref=kv_part(peer, g, h), dst_ref=kvbuf.at[g, mine[h], :, pl.ds(row0, tokens), :],
                    send_sem=kv_send.at[g, d - 1, h], recv_sem=kv_recv.at[g, d - 1, h],
                    device_id={"head": peer}, device_id_type=MESH)
                copy.start()
                kv_copies[g].append(copy)
    for g in range(groups):
        for d in range(1, heads):
            peer = (me_h + d) % heads
            copy = pltpu.make_async_remote_copy(
                src_ref=q_part(peer, g), dst_ref=qbuf.at[g, :, pl.ds(row0, tokens), :],
                send_sem=q_send.at[g, d - 1], recv_sem=q_recv.at[g, d - 1],
                device_id={"head": peer}, device_id_type=MESH)
            copy.start()
            q_copies[g].append(copy)

    def member_at(d, distance):
        return ring_member((place + n - distance) % n if d == 0 else (place + distance) % n, n)

    def hop(g, d, t, h):
        origin = member_at(d, t)
        block = origin if h == 0 else 2 * n - 1 - origin
        return pltpu.make_async_remote_copy(
            src_ref=kvbuf.at[g, block], dst_ref=kvbuf.at[g, block],
            send_sem=ring_send.at[g, d, t, h], recv_sem=ring_recv.at[g, d, t, h],
            device_id={"ctx": right if d == 0 else left}, device_id_type=MESH)

    def arrived(g, d, t):
        for h in range(2):
            hop(g, d, t, h).wait_recv()

    def forward(g, d, t):
        for h in range(2):
            hop(g, d, t - 1, h).wait_recv()
            hop(g, d, t, h).start()

    factor = HEAD_WIDTH ** -0.5 * math.log2(math.e)
    pair = 4
    tiles, rows = per_group // pair, pair * span

    def doc_of(block):
        end, found = jnp.int32(0), jnp.int32(0)
        for j in range(docs_ref.shape[0]):
            end = end + docs_ref[j]
            found = found + jnp.where(end <= block, 1, 0).astype(jnp.int32)
        return found

    def scores_of(g, hq, t, keys):
        base = t * pair * HEAD_WIDTH
        queries = jnp.concatenate(
            [qbuf[g, hq, :, base + j * HEAD_WIDTH: base + (j + 1) * HEAD_WIDTH] for j in range(pair)], axis=0)
        return lax.dot_general(queries, keys, (((1,), (1,)), ((), ())), preferred_element_type=jnp.float32)

    def mix(p, values):
        return lax.dot_general(p.astype(jnp.bfloat16), values, (((1,), (0,)), ((), ())),
                               preferred_element_type=jnp.float32)

    def fold(g, hq, *blocks):
        doc = doc_of(jnp.where(hq == 0, mine[0], mine[1]))
        shifts = [jnp.where(doc_of(block) == doc, jnp.float32(0), jnp.float32(-LOW)) for block in blocks]
        keys = jnp.concatenate([kvbuf[g, block, 0] for block in blocks], axis=0)
        values = jnp.concatenate([kvbuf[g, block, 1] for block in blocks], axis=0)
        for t in range(tiles):
            s = scores_of(g, hq, t, keys)
            m_old = m_ref[hq, t]
            parts = [s[:, i * span:(i + 1) * span] for i in range(len(blocks))]
            top = parts[0] - shifts[0]
            for part, shift in zip(parts[1:], shifts[1:]):
                top = jnp.maximum(top, part - shift)
            m = jnp.maximum(m_old, jnp.max(top, axis=-1, keepdims=True))
            parts = [jnp.exp2((part - (m + shift)) * factor) for part, shift in zip(parts, shifts)]
            p = jnp.concatenate(parts, axis=1)
            alpha = jnp.exp2((m_old - m) * factor)
            m_ref[hq, t] = m
            l_ref[hq, t] = l_ref[hq, t] * alpha + sum(parts)
            acc_ref[hq, t] = acc_ref[hq, t] * alpha + mix(p, values)

    def diagonal(g):
        def each(hq, carry):
            block = jnp.where(hq == 0, mine[0], mine[1])
            keys, values = kvbuf[g, block, 0], kvbuf[g, block, 1]
            row_at = lax.broadcasted_iota(jnp.int32, (rows, span), 0) % span
            seen = lax.broadcasted_iota(jnp.int32, (rows, span), 1) <= row_at
            for t in range(tiles):
                s = jnp.where(seen, scores_of(g, hq, t, keys), LOW)
                m = jnp.max(s, axis=-1, keepdims=True)
                p = jnp.exp2((s - m) * factor)
                m_ref[hq, t] = jnp.broadcast_to(m, (rows, span))
                l_ref[hq, t] = p
                acc_ref[hq, t] = mix(p, values)
            return carry

        lax.fori_loop(0, 2, each, 0)
        fold(g, 1, mine[0])

    def absorb(g, ways, t):
        origins = [member_at(way, t + 1) for way in ways]
        fold(g, 1, *origins)

        def each(k, carry):
            origin = jnp.where(k == 0, origins[0], origins[-1])
            lower = origin < me_c
            fold(g, jnp.where(lower, 0, 1), jnp.where(lower, origin, 2 * n - 1 - origin))
            return carry

        lax.fori_loop(0, len(ways), each, 0)

    back = []

    def finish(g):
        cols = pl.ds(pl.multiple_of((me_h * groups + g) * width, width), width)
        for hq in range(2):
            for t in range(tiles):
                out = acc_ref[hq, t] / jnp.sum(l_ref[hq, t], axis=-1, keepdims=True)
                out = out.astype(obuf.dtype)
                for j in range(pair):
                    base = (t * pair + j) * HEAD_WIDTH
                    obuf[g, hq, :, base:base + HEAD_WIDTH] = out[j * span:(j + 1) * span]
            place_out = out_ref.at[0, hq, :, cols]
            for d in range(1, heads):
                peer = (me_h + d) % heads
                copy = pltpu.make_async_remote_copy(
                    src_ref=obuf.at[g, hq, pl.ds(pl.multiple_of(peer * tokens, tokens), tokens), :],
                    dst_ref=place_out, send_sem=o_send.at[g, hq, d - 1], recv_sem=o_recv.at[g, hq, d - 1],
                    device_id={"head": peer}, device_id_type=MESH)
                copy.start()
                back.append(copy)
            copy = pltpu.make_async_copy(obuf.at[g, hq, pl.ds(row0, tokens), :], place_out,
                                         own_sem.at[3 * groups + 2 * g + hq])
            copy.start()
            back.append(copy)

    def ready(g):
        for h in range(2):
            own[3 * g + h].wait()
        for copy in kv_copies[g]:
            copy.wait_recv()
        for d in range(2):
            for h in range(2):
                hop(g, d, 0, h).start()

    def queries_ready(g):
        own[3 * g + 2].wait()
        for copy in q_copies[g]:
            copy.wait_recv()

    both, two = (0, 1), groups == 2
    for g in range(groups):
        ready(g)
    forward(0, 0, 1)
    forward(0, 1, 1)
    queries_ready(0)
    diagonal(0)

    def early(t, carry):
        forward(0, 0, t)
        forward(0, 1, t)
        absorb(0, both, t - 2)
        return carry

    lax.fori_loop(2, half - 1, early, 0)
    forward(0, 0, half - 1)
    if two:
        forward(1, 1, 1)
    absorb(0, both, half - 3)
    if two:
        forward(1, 0, 1)
        forward(1, 1, 2)
    arrived(0, 1, half - 2)
    absorb(0, both, half - 2)
    arrived(0, 0, half - 1)
    if two:
        forward(1, 0, 2)
        forward(1, 1, 3)
    absorb(0, (0,), half - 1)
    finish(0)

    def late(t, carry):
        forward(1, 0, t)
        forward(1, 1, t + 1)
        absorb(1, both, t - 3)
        return carry

    if two:
        queries_ready(1)
        diagonal(1)
        lax.fori_loop(3, half - 1, late, 0)
        absorb(1, both, half - 4)
        absorb(1, both, half - 3)
        arrived(1, 0, half - 2)
        absorb(1, both, half - 2)
        arrived(1, 1, half - 1)
        absorb(1, (1,), half - 1)
        finish(1)

    for g in range(groups):
        for copy in kv_copies[g] + q_copies[g]:
            copy.wait_send()
        for d in range(2):
            for t in range(half if d == g else half - 1):
                for h in range(2):
                    hop(g, d, t, h).wait_send()
    for copy in back:
        copy.wait()


def local(query, keyval, doc_blocks):
    n, heads = lax.axis_size("ctx"), lax.axis_size("head")
    tokens = query.shape[2]
    span = tokens * heads
    groups, per_group = keyval.shape[4] // heads // HEAD_WIDTH, QUERY_HEADS // KEY_VALUE_HEADS
    width = per_group * HEAD_WIDTH
    assert span == BLK and groups in (1, 2) and n % 2 == 0 and n >= 8
    kind = query.dtype
    anywhere = pl.BlockSpec(memory_space=pl.ANY)
    dma = pltpu.SemaphoreType.DMA
    state = pltpu.VMEM((2, per_group // 4, 4 * span, HEAD_WIDTH), jnp.float32)
    return pl.pallas_call(
        functools.partial(fused_kernel, n, heads, per_group),
        out_shape=jax.ShapeDtypeStruct(query.shape, kind),
        in_specs=[pl.BlockSpec(memory_space=pltpu.SMEM), anywhere, anywhere],
        out_specs=anywhere,
        scratch_shapes=[
            pltpu.VMEM((groups, 2, span, width), kind),
            pltpu.VMEM((groups, 2 * n, 2, span, HEAD_WIDTH), kind),
            pltpu.VMEM((groups, 2, span, width), kind),
            state, state, state,
            dma((5 * groups,)),
            dma((groups, heads - 1)), dma((groups, heads - 1)),
            dma((groups, heads - 1, 2)), dma((groups, heads - 1, 2)),
            dma((groups, 2, n // 2, 2)), dma((groups, 2, n // 2, 2)),
            dma((groups, 2, heads - 1)), dma((groups, 2, heads - 1)),
        ],
        compiler_params=pltpu.CompilerParams(collective_id=0, has_side_effects=True),
        name="fused",
    )(doc_blocks, query, keyval)


def solution(mesh):
    placed = (P("ctx", None, "head", None), P("ctx", None, None, "head", None), P())
    return jax.shard_map(
        local, mesh=mesh, in_specs=placed, out_specs=P("ctx", None, "head", None), check_vma=False
    )
```
